32 devices in a mesh: parts: 2 (over y), tm: 4 (over z), space: 2 (over x), spin: 2 (over core).
Axes of the slice: x: 2, y: 2, z: 4, core: 2. Of those that a mesh axis runs over, the one named last changes fastest.
Arguments:
- eigenvectors: float32 [2, 8, 3, 512, 256], P(None, ('parts', 'tm'), None, ('space', 'spin')), parts along dimension 1, may hold values from -0.25 to 0.25
- displaced: float32 [2, 3, 8, 3, 512, 256], P(None, None, ('parts', 'tm'), None, ('space', 'spin')), parts along dimension 2, may hold values from -0.25 to 0.25
- perambulators: float32 [2, 8, 4, 256, 256], P(None, 'parts', 'spin', 'space', 'tm'), parts along dimension 1, may hold values from -6 to 6
- gamma_values: float32 [2, 4, 4, 4], replicated, may hold values from -4 to 4
- spin_pattern: int32 [4, 4, 4], replicated, may hold values 0 or 1
- directions: int32 [4], replicated, may hold values from 0 to 2, as said below
- momenta: int32 [4], replicated, may hold values from 0 to 3
Outputs:
- products: float32 [2, 4, 8, 4, 256, 256], P(None, None, ('parts', 'tm'), 'spin', 'space'), parts along dimension 2
The draws below stay inside these ranges and needn't reach their ends.
There are 2 independent parts, one for each index of `parts`. The reference program is written for one: setup_inputs(seed, part) draws one part's arguments, and reference() takes and returns one part's arrays. A program takes and returns all parts, laid end to end along the dimension named above; an argument that names none is the same for every part. Nothing has to cross between parts.
Inputs may be any that keep to these rules, and one draw needn't show every extreme that they name: Every one of the 3 directions is named by some operator.
All inputs are finite; a program needn't handle non-finite values.
Results may differ from the reference program's by a relative error of at most 0.0001.
Values sent between devices are 32-bit elements; how exact they have to be, the bound alone decides.
No kernel may reach another device: no remote copies, remote signals or barrier semaphores. Data moves between devices by JAX's collectives and lax.ppermute only.
A program may use at most 64 MiB of HBM per device.

```python
import math
import jax
import jax.numpy as jnp
from jax import lax

K = 256
SRC = 256
NSPIN = 4
NOP = 4
NDIR = 3
NMOM = 4
NT = 4
NSITES = 512
PLANE = 256
LZ = 2


def draw_directions(key, part):
    first = jax.random.permutation(jax.random.fold_in(key, 11), NDIR).astype(jnp.int32)
    extra = jax.random.randint(jax.random.fold_in(key, 12), (NOP - NDIR,), 0, NDIR).astype(jnp.int32)
    return jnp.concatenate([first, extra]).astype(jnp.int32)


def touch_ends(result, own_key, least, top_value):
    place = [jax.random.randint(jax.random.fold_in(own_key, axis), (), 0, length) for axis, length in enumerate(result.shape)]
    longest = result.shape.index(max(result.shape))
    neighbour = place[:longest] + [(place[longest] + 1) % result.shape[longest]] + place[longest + 1:]
    return result.at[tuple(place)].set(least).at[tuple(neighbour)].set(top_value)


def block_scale(key, dims, split, least, largest):
    factor_of, own = 1.0, jax.random.fold_in(key, 6)
    for dim, shards_of in split:
        draws = jnp.exp(jax.random.uniform(jax.random.fold_in(own, dim), (shards_of,), jnp.float32, least / len(split), largest / len(split)))
        factor_of = factor_of * jnp.repeat(draws, dims[dim] // shards_of).reshape([-1 if axis == dim else 1 for axis in range(len(dims))])
    return factor_of


def scatter_about(key, dims, width, bound, cuts=(), kind=jnp.bfloat16):
    gain = block_scale(key, dims, cuts, -0.22, 0.18) if cuts else 1.0
    values = jax.random.normal(key, dims, jnp.float32) * width * gain
    return jnp.minimum(jnp.maximum(values, -bound), bound).astype(kind)


def setup_inputs(seed: int = 0, part: int = 0) -> dict:
    key_list = jax.random.split(jax.random.key(seed), 8)
    part_keys = jax.random.split(jax.random.fold_in(key_list[7], part), 8)
    eigenvectors = scatter_about(part_keys[0], (2, NT, 3, NSITES, K), NSITES ** -0.5, 0.25, ((1, 4), (3, 4)), jnp.float32)
    displaced = scatter_about(part_keys[1], (2, NDIR, NT, 3, NSITES, K), NSITES ** -0.5, 0.25, ((2, 4), (4, 4)), jnp.float32)
    perambulators = scatter_about(part_keys[2], (2, NT, NSPIN, K, SRC), 1.0, 6.0, ((2, 2), (3, 2), (4, 4)), jnp.float32)
    gamma_values = scatter_about(key_list[3], (2, NOP, NSPIN, NSPIN), 0.7, 4.0, (), jnp.float32)
    spin_pattern = touch_ends((jax.random.randint(key_list[4], (NOP, NSPIN, NSPIN), 0, 2) < 1).astype(jnp.int32), jax.random.fold_in(key_list[4], 1), 0, 1)
    directions = draw_directions(jax.random.fold_in(key_list[7], 71), part)
    momenta = touch_ends(jax.random.randint(key_list[6], (NOP,), 0, NMOM), jax.random.fold_in(key_list[6], 1), 0, NMOM - 1).astype(jnp.int32)
    return {"eigenvectors": eigenvectors, "displaced": displaced, "perambulators": perambulators, "gamma_values": gamma_values, "spin_pattern": spin_pattern, "directions": directions, "momenta": momenta}


highest = lax.Precision.HIGHEST


def reference(eigenvectors, displaced, perambulators, gamma_values, spin_pattern, directions, momenta):
    sites = jnp.arange(NSITES, dtype=jnp.int32)
    third = sites // PLANE
    angles = ((momenta[:, None] * third[None, :]) % LZ).astype(jnp.float32) * (2.0 * math.pi / LZ)
    cosine = jnp.cos(angles)
    sine = jnp.sin(angles)
    spin_matrix = gamma_values * spin_pattern.astype(jnp.float32)[None]

    def per_time(tslice):
        vectors = lax.dynamic_index_in_dim(eigenvectors, tslice, 1, keepdims=False)
        left = vectors.reshape(-1, K)
        rows = []
        for operator in range(NOP):
            moved = lax.dynamic_index_in_dim(displaced, directions[operator], 1, keepdims=False)
            moved = lax.dynamic_index_in_dim(moved, tslice, 1, keepdims=False)
            cos_row = cosine[operator][:, None]
            sin_row = sine[operator][:, None]
            real_w = cos_row * moved[0] + sin_row * moved[1]
            imag_w = cos_row * moved[1] - sin_row * moved[0]
            right = jnp.concatenate([jnp.stack([real_w, imag_w]), jnp.stack([imag_w, -real_w])], axis=-1).reshape(-1, 2 * K)
            elem = lax.dot_general(left, right, (((0,), (0,)), ((), ())), precision=highest, preferred_element_type=jnp.float32)
            rows.append(elem.reshape(K, 2, K))
        elementals = jnp.stack(rows)
        real_e = elementals[:, :, 0]
        imag_e = elementals[:, :, 1]
        peram = lax.dynamic_index_in_dim(perambulators, tslice, 1, keepdims=False)
        real_q = jnp.einsum('oab,bls->oals', spin_matrix[0], peram[0], precision=highest) - jnp.einsum('oab,bls->oals', spin_matrix[1], peram[1], precision=highest)
        imag_q = jnp.einsum('oab,bls->oals', spin_matrix[0], peram[1], precision=highest) + jnp.einsum('oab,bls->oals', spin_matrix[1], peram[0], precision=highest)
        real_r = jnp.einsum('okl,oals->oaks', real_e, real_q, precision=highest) - jnp.einsum('okl,oals->oaks', imag_e, imag_q, precision=highest)
        imag_r = jnp.einsum('okl,oals->oaks', real_e, imag_q, precision=highest) + jnp.einsum('okl,oals->oaks', imag_e, real_q, precision=highest)
        return jnp.stack([real_r, imag_r])

    results = lax.map(per_time, jnp.arange(NT, dtype=jnp.int32))
    return jnp.transpose(results, (1, 2, 0, 3, 4, 5))
```

```python
import functools
import math

import numpy as np

import jax
import jax.numpy as jnp
from jax import lax
from jax.experimental import pallas as pl
from jax.experimental.pallas import tpu as pltpu
from jax.sharding import PartitionSpec as P

f32 = jnp.float32
bf16 = jnp.bfloat16
VMEM = pl.BlockSpec(memory_space=pltpu.VMEM)
SMEM = pl.BlockSpec(memory_space=pltpu.SMEM)


def cut(value):
    high = value.astype(bf16)
    return high, (value - high.astype(f32)).astype(bf16)


def place(bits):
    return jnp.stack([lax.axis_index(axis) for axis in bits]).astype(jnp.int32)


def partner(value, axis, distance):
    size = lax.axis_size(axis)
    return lax.ppermute(value, axis, [(i, i ^ distance) for i in range(size)])


def pack_body(where, peram, *outs):
    for distance, out in enumerate(outs):
        for part in range(peram.shape[0]):
            out[part] = peram[part, where[1] ^ distance]


def pack(where, peram):
    parts, times = peram.shape[:2]
    shape = jax.ShapeDtypeStruct((parts,) + peram.shape[2:], f32)
    return pl.pallas_call(
        pack_body,
        out_shape=[shape] * times,
        in_specs=[SMEM, VMEM],
        out_specs=[VMEM] * times,
        name="pack",
        cost_estimate=pl.CostEstimate(flops=0, bytes_accessed=peram.size * 8, transcendentals=0),
        compiler_params=pltpu.CompilerParams(vmem_limit_bytes=8 << 20),
    )(where, peram)


def sums_body(chips, cores, where, vectors, moved, own, keep, send, left_high, left_low):
    colours, sites, width = vectors.shape[2:]
    depth = colours * sites

    @pl.when(pl.program_id(0) == 0)
    def _():
        for colour in range(colours):
            at = colour * sites
            real = vectors[0, 0, colour].T
            imag = vectors[1, 0, colour].T
            for row, first, value in (
                (0, 0, real),
                (0, depth, imag),
                (width, 0, -imag),
                (width, depth, real),
            ):
                high, low = cut(value)
                left_high[row : row + width, first + at : first + at + sites] = high
                left_low[row : row + width, first + at : first + at + sites] = low

    right = jnp.concatenate([moved[part, 0, 0, colour] for part in range(2) for colour in range(colours)])
    high, low = cut(right)
    rows = width // (chips * cores)

    def product(start, count):
        a_high = left_high[pl.ds(start, count), :]
        a_low = left_low[pl.ds(start, count), :]
        dot = functools.partial(jnp.dot, preferred_element_type=f32)
        return dot(a_high, high) + dot(a_high, low) + dot(a_low, high)

    for part in range(2):
        base = part * width
        first = pl.multiple_of(base + where[2] * cores * rows, cores * rows)
        own[0, part] = product(first, cores * rows)
        for away in range(1, chips):
            chip = where[2] ^ away
            for core, out in ((0, keep), (1, send)):
                start = pl.multiple_of(base + (chip * cores + (where[3] ^ core)) * rows, rows)
                out[0, away - 1, part] = product(start, rows)


def sums(where, vectors, displaced, chips, cores):
    colours, sites, width = vectors.shape[2:]
    kinds = displaced.shape[1]
    rows = width // (chips * cores)
    depth = 2 * colours * sites
    own = jax.ShapeDtypeStruct((kinds, 2, rows * cores, width), f32)
    other = jax.ShapeDtypeStruct((kinds, chips - 1, 2, rows, width), f32)
    return pl.pallas_call(
        functools.partial(sums_body, chips, cores),
        out_shape=[own, other, other],
        grid=(kinds,),
        in_specs=[
            SMEM,
            pl.BlockSpec(vectors.shape, lambda i: (0,) * 5, pipeline_mode=pl.Buffered(1)),
            pl.BlockSpec((2, 1) + displaced.shape[2:], lambda i: (0, i, 0, 0, 0, 0)),
        ],
        out_specs=[
            pl.BlockSpec((1,) + own.shape[1:], lambda i: (i, 0, 0, 0)),
            pl.BlockSpec((1,) + other.shape[1:], lambda i: (i, 0, 0, 0, 0)),
            pl.BlockSpec((1,) + other.shape[1:], lambda i: (i, 0, 0, 0, 0)),
        ],
        scratch_shapes=[pltpu.VMEM((2 * width, depth), bf16)] * 2,
        name="sums",
        cost_estimate=pl.CostEstimate(
            flops=12 * width * depth * width * kinds,
            bytes_accessed=4 * (vectors.size + displaced.size) + 4 * kinds * 4 * width * width,
            transcendentals=0,
        ),
        compiler_params=pltpu.CompilerParams(vmem_limit_bytes=24 << 20, dimension_semantics=("arbitrary",)),
    )(where, vectors, displaced)


def phase(turns, chips, table):
    value = f32(table[0])
    for step in range(1, chips):
        value = jnp.where(turns == step, f32(table[step]), value)
    return value


def products_body(
    chips, cores, half, tables, where, gamma, pattern, directions, momenta, mine, theirs, *rest
):
    away_count = chips - 1
    far = rest[:away_count]
    far_other = rest[away_count : 2 * away_count]
    rest = rest[2 * away_count :]
    blocks = rest[: half * chips * cores]
    rest = rest[half * chips * cores :]
    if len(rest) == 5:
        rest = rest[1:]
    out, spread, e_high, e_low = rest
    operator = pl.program_id(0)
    row_count, width = mine.shape[2:]
    per_core, cols, depth_rows = blocks[0].shape[1:]

    @pl.when(operator == 0)
    def _():
        for step in range(half):
            at = pl.multiple_of(((where[1] ^ step) & (half - 1)) * cols, cols)
            for away in range(chips):
                for core in range(cores):
                    block = blocks[(step * chips + away) * cores + core]
                    for part in range(2):
                        for spin in range(per_core):
                            spread[
                                part,
                                core * per_core + spin,
                                pl.ds(at, cols),
                                away * depth_rows : (away + 1) * depth_rows,
                            ] = block[part, spin]

    kind = directions[operator]
    real = jnp.zeros((row_count, width), f32)
    imag = jnp.zeros((row_count, width), f32)
    for away in range(chips):
        turns = lax.rem(momenta[operator] * (where[2] ^ away), chips)
        cosine = phase(turns, chips, tables[0])
        sine = phase(turns, chips, tables[1])
        if away == 0:
            pair = [mine[kind, part] + theirs[kind, part] for part in range(2)]
        else:
            here = [far[away - 1][kind, part] for part in range(2)]
            there = [far_other[away - 1][kind, part] for part in range(2)]
            first = where[3] == 0
            pair = [
                jnp.concatenate([jnp.where(first, a, b), jnp.where(first, b, a)])
                for a, b in zip(here, there)
            ]
        real = real + cosine * pair[0] + sine * pair[1]
        imag = imag + cosine * pair[1] - sine * pair[0]
    lane = lax.broadcasted_iota(jnp.int32, (row_count, width), 1)
    bit = 1
    while bit < chips:
        reach = bit * depth_rows
        turned = []
        for value in (real, imag):
            up = pltpu.roll(value, width - reach, 1)
            down = up if 2 * reach == width else pltpu.roll(value, reach, 1)
            swapped = jnp.where((lane & reach) == 0, up, down)
            turned.append(jnp.where((where[2] & bit) != 0, swapped, value))
        real, imag = turned
        bit *= 2
    for value, sign, spots in (
        (real, 1.0, ((0, 0), (row_count, width))),
        (imag, 1.0, ((row_count, 0),)),
        (imag, -1.0, ((0, width),)),
    ):
        high, low = cut(sign * value)
        for row, col in spots:
            e_high[row : row + row_count, col : col + width] = high
            e_low[row : row + row_count, col : col + width] = low

    sinks = out.shape[3]
    mixed = []
    for sink in range(sinks):
        row = where[3] * sinks + sink
        mixed_real = None
        mixed_imag = None
        for core in range(cores):
            for spin in range(per_core):
                source = (where[3] ^ core) * per_core + spin
                on = pattern[operator, row, source].astype(f32)
                g_real = gamma[0, operator, row, source] * on
                g_imag = gamma[1, operator, row, source] * on
                p_real = spread[0, core * per_core + spin]
                p_imag = spread[1, core * per_core + spin]
                one = g_real * p_real - g_imag * p_imag
                two = g_real * p_imag + g_imag * p_real
                mixed_real = one if mixed_real is None else mixed_real + one
                mixed_imag = two if mixed_imag is None else mixed_imag + two
        mixed.append(jnp.concatenate([mixed_real, mixed_imag], axis=1))
    high, low = cut(jnp.concatenate(mixed))

    def dot(left, right):
        return lax.dot_general(left, right, (((1,), (1,)), ((), ())), preferred_element_type=f32)

    result = dot(e_high[...], high) + dot(e_high[...], low) + dot(e_low[...], high)
    lanes = out.shape[5]
    for sink in range(sinks):
        out[0, 0, 0, sink] = result[:row_count, sink * lanes : (sink + 1) * lanes]
        out[1, 0, 0, sink] = result[row_count:, sink * lanes : (sink + 1) * lanes]


def products(side, where, scalars, mine, theirs, far, far_other, blocks, shape, chips, cores, previous):
    half = len(blocks) // (chips * cores)
    width = mine.shape[-1]
    spins = scalars[0].shape[2]
    lanes = shape[-1] // 2
    rows = mine.shape[2]
    times = 2 * half
    tables = [
        [float(v) for v in fn(np.arange(chips, dtype=np.float32) * np.float32(2.0 * math.pi / chips))]
        for fn in (np.cos, np.sin)
    ]
    operands = [where, *scalars, mine, theirs, *far, *far_other, *blocks]
    specs = [SMEM] * 5 + [VMEM] * (len(operands) - 5)
    aliases = {}
    if previous is not None:
        aliases = {len(operands): 0}
        operands.append(previous)
        specs.append(pl.BlockSpec(memory_space=pl.ANY))
    specs = [
        pl.BlockSpec(memory_space=s.memory_space) if s is not SMEM else s for s in specs
    ]
    return pl.pallas_call(
        functools.partial(products_body, chips, cores, half, tables),
        out_shape=jax.ShapeDtypeStruct(shape, f32),
        grid_spec=pltpu.PrefetchScalarGridSpec(
            num_scalar_prefetch=1,
            grid=(shape[1],),
            in_specs=specs[1:],
            out_specs=pl.BlockSpec(
                (2, 1, 1) + shape[3:5] + (lanes,),
                lambda o, where: (0, o, 0, 0, 0, (where[1] // half) ^ side),
            ),
            scratch_shapes=[
                pltpu.VMEM((2, spins, lanes, width), f32),
                pltpu.VMEM((2 * rows, 2 * width), bf16),
                pltpu.VMEM((2 * rows, 2 * width), bf16),
            ],
        ),
        input_output_aliases=aliases,
        name=f"products_{side}",
        cost_estimate=pl.CostEstimate(
            flops=3 * 2 * shape[1] * shape[3] * 2 * rows * 2 * width * lanes,
            bytes_accessed=4 * math.prod(shape) // 2,
            transcendentals=0,
        ),
        compiler_params=pltpu.CompilerParams(vmem_limit_bytes=24 << 20, dimension_semantics=("arbitrary",)),
    )(*operands)


def local(eigenvectors, displaced, perambulators, gamma_values, spin_pattern, directions, momenta):
    width = eigenvectors.shape[4]
    operators = gamma_values.shape[1]
    spins = gamma_values.shape[2]
    times = lax.axis_size("tm")
    chips = lax.axis_size("space")
    cores = lax.axis_size("spin")
    where = place(("parts", "tm", "space", "spin"))
    half = times // 2

    mine_blocks = pack(where, jnp.swapaxes(perambulators, 3, 4))
    near = [mine_blocks[0]] + [partner(mine_blocks[d], "tm", d) for d in range(1, times)]
    own, keep, send = sums(where, eigenvectors, displaced, chips, cores)
    far_sum = keep + partner(send, "spin", 1)
    theirs = partner(own, "spin", 1)
    far = [partner(far_sum[:, away - 1], "space", away) for away in range(1, chips)]
    far_other = [partner(value, "spin", 1) for value in far]
    gathered = []
    for d in range(times):
        chip_blocks = [near[d]] + [partner(near[d], "space", away) for away in range(1, chips)]
        gathered.append([(block, partner(block, "spin", 1)) for block in chip_blocks])

    scalars = [gamma_values, spin_pattern, directions, momenta]
    shape = (2, operators, eigenvectors.shape[1], spins // cores, width // chips, perambulators.shape[4] * times)
    result = None
    for side in range(2):
        blocks = [
            block
            for d in range(side * half, (side + 1) * half)
            for pair in gathered[d]
            for block in pair
        ]
        result = products(side, where, scalars, own, theirs, far, far_other, blocks, shape, chips, cores, result)
    return result


def solution(mesh):
    in_specs = (
        P(None, ("parts", "tm"), None, ("space", "spin"), None),
        P(None, None, ("parts", "tm"), None, ("space", "spin"), None),
        P(None, "parts", "spin", "space", "tm"),
        P(),
        P(),
        P(),
        P(),
    )
    out_specs = P(None, None, ("parts", "tm"), "spin", "space", None)
    return jax.shard_map(local, mesh=mesh, in_specs=in_specs, out_specs=out_specs, check_vma=False)
```

```python
import functools
import math

import numpy as np

import jax
import jax.numpy as jnp
from jax import lax
from jax.experimental import pallas as pl
from jax.experimental.pallas import tpu as pltpu
from jax.sharding import PartitionSpec as P


f32 = jnp.float32
bf16 = jnp.bfloat16
VMEM = pl.BlockSpec(memory_space=pltpu.VMEM)
SMEM = pl.BlockSpec(memory_space=pltpu.SMEM)
HBM = pl.BlockSpec(memory_space=pltpu.HBM)


def in_hbm(value):
    return pltpu.with_memory_space_constraint(value, pltpu.HBM)


def cut(value):
    high = value.astype(bf16)
    return high, (value - high.astype(f32)).astype(bf16)


def three_pass(left, right, dims):
    def dot(a, b):
        return lax.dot_general(a, b, (dims, ((), ())), preferred_element_type=f32)

    return dot(left[0], right[0]) + dot(left[0], right[1]) + dot(left[1], right[0])


def place(axes):
    return jnp.stack([lax.axis_index(axis) for axis in axes]).astype(jnp.int32)


def partner(value, axis, distance):
    size = lax.axis_size(axis)
    return lax.ppermute(value, axis, [(i, i ^ distance) for i in range(size)])


def pack_body(first, where, peram, together, *rest):
    outs, sems = rest[:-1], rest[-1]
    copies = []
    for distance, out in enumerate(outs):
        tslice = where[1] ^ distance
        targets = [out]
        if distance in first:
            targets.append(together.at[first.index(distance)])
        for target in targets:
            copies.append(pltpu.make_async_copy(peram.at[:, tslice], target, sems.at[len(copies)]))
            copies[-1].start()
    for copy in copies:
        copy.wait()


def pack(where, peram, first):
    parts, times = peram.shape[:2]
    one = (parts,) + peram.shape[2:]
    return pl.pallas_call(
        functools.partial(pack_body, first),
        out_shape=[jax.ShapeDtypeStruct(dims, f32) for dims in [(len(first),) + one] + [one] * times],
        in_specs=[SMEM, HBM],
        out_specs=[VMEM] * (times + 1),
        scratch_shapes=[pltpu.SemaphoreType.DMA((times + len(first),))],
        name="pack",
        cost_estimate=pl.CostEstimate(flops=0, bytes_accessed=peram.size * 12, transcendentals=0),
        compiler_params=pltpu.CompilerParams(vmem_limit_bytes=8 << 20),
    )(where, in_hbm(peram))


def sums_body(
    chips, cores, where, vectors, moved, v_other, d_other, own, other, v_buf, d_buf, left_high, left_low, v_sem, d_sem
):
    colours, sites, width = vectors.shape[2:]
    kinds = moved.shape[1]
    depth = colours * sites
    rows = width // (chips * cores)
    kind = pl.program_id(0)

    def v_copy(colour):
        return pltpu.make_async_copy(vectors.at[:, 0, colour], v_buf.at[colour], v_sem.at[colour])

    def d_copy(index):
        return pltpu.make_async_copy(moved.at[:, index, 0], d_buf.at[index], d_sem.at[index])

    @pl.when(kind == 0)
    def _():
        for colour in range(colours):
            v_copy(colour).start()
        for index in range(kinds):
            d_copy(index).start()
        spots = [(chip ^ where[2]) * rows for chip in range(chips)]
        for source in range(cores - 1, -1, -1):
            for colour in range(colours):
                if source == 0:
                    v_copy(colour).wait()
                    pair = v_buf[colour, 0].T, v_buf[colour, 1].T
                else:
                    pair = v_other[0, 0, colour].T, v_other[1, 0, colour].T
                at = source * 2 * depth + colour * sites
                for chip, spot in enumerate(spots):
                    base = chip * cores * rows
                    real, imag = [
                        jnp.where(where[3] == 0, value[base : base + rows], value[base + rows : base + 2 * rows])
                        for value in pair
                    ]
                    for scratch, re, im in zip((left_high, left_low), cut(real), cut(imag)):
                        for part, col, value in ((0, at, re), (0, depth + at, im), (1, at, -im), (1, depth + at, re)):
                            to = pl.multiple_of(part * chips * rows + spot, rows)
                            scratch[pl.ds(to, rows), col : col + sites] = value

    d_copy(kind).wait()
    result = None
    for source in range(cores):
        value = d_buf[kind] if source == 0 else d_other[:, kind, 0]
        at = slice(source * 2 * depth, (source + 1) * 2 * depth)
        term = three_pass((left_high[:, at], left_low[:, at]), cut(value.reshape(2 * depth, width)), ((1,), (0,)))
        result = term if result is None else result + term
    for part in range(2):
        at = part * chips * rows
        own[0, part] = result[at : at + rows]
        for away in range(chips - 1):
            at += rows
            other[0, away, part] = result[at : at + rows]


def sums(where, vectors, displaced, v_other, d_other, chips, cores):
    colours, sites, width = vectors.shape[2:]
    kinds = displaced.shape[1]
    rows = width // (chips * cores)
    depth = 2 * colours * sites
    own = jax.ShapeDtypeStruct((kinds, 2, rows, width), f32)
    other = jax.ShapeDtypeStruct((kinds, chips - 1, 2, rows, width), f32)
    return pl.pallas_call(
        functools.partial(sums_body, chips, cores),
        out_shape=[own, other],
        grid=(kinds,),
        in_specs=[SMEM, HBM, HBM, VMEM, VMEM],
        out_specs=[
            pl.BlockSpec((1,) + own.shape[1:], lambda i: (i, 0, 0, 0)),
            pl.BlockSpec((1,) + other.shape[1:], lambda i: (i, 0, 0, 0, 0)),
        ],
        scratch_shapes=[
            pltpu.VMEM((colours, 2, sites, width), f32),
            pltpu.VMEM((kinds, 2, colours, sites, width), f32),
            pltpu.VMEM((2 * chips * rows, cores * depth), bf16),
            pltpu.VMEM((2 * chips * rows, cores * depth), bf16),
            pltpu.SemaphoreType.DMA((colours,)),
            pltpu.SemaphoreType.DMA((kinds,)),
        ],
        name="sums",
        cost_estimate=pl.CostEstimate(
            flops=12 * width * depth * width * kinds,
            bytes_accessed=4 * (vectors.size + displaced.size) + 4 * kinds * 4 * width * width,
            transcendentals=0,
        ),
        compiler_params=pltpu.CompilerParams(vmem_limit_bytes=20 << 20, dimension_semantics=("arbitrary",)),
    )(where, in_hbm(vectors), in_hbm(displaced), v_other, d_other)


def mix_body(cores, where, gamma, pattern, mine, theirs, out_high, out_low, spread):
    operator = pl.program_id(0)
    times = mine.shape[0]
    per_core, cols, rows = mine.shape[2:]
    lanes = times * cols
    spins = cores * per_core
    sinks = spins // cores

    @pl.when(operator == 0)
    def _():
        for step in range(times):
            at = pl.multiple_of((where[1] ^ step) * cols, cols)
            for core, block in enumerate((mine, theirs)):
                for spin in range(per_core):
                    real = block[step, 0, spin]
                    imag = block[step, 1, spin]
                    for part, value in enumerate((real, imag, real + imag)):
                        spread[part, core * per_core + spin, pl.ds(at, cols), :] = value

    for sink in range(sinks):
        row = where[3] * sinks + sink
        totals = [None] * 3
        for core in range(cores):
            for spin in range(per_core):
                source = (where[3] ^ core) * per_core + spin
                on = pattern[operator, row, source].astype(f32)
                a = gamma[0, operator, row, source] * on
                b = gamma[1, operator, row, source] * on
                for index, (factor, part) in enumerate(((a, 2), (b - a, 0), (a + b, 1))):
                    term = factor * spread[part, core * per_core + spin]
                    totals[index] = term if totals[index] is None else totals[index] + term
        for part, value in enumerate((totals[0] - totals[2], totals[0] + totals[1])):
            high, low = cut(value)
            at = (slice(sink * lanes, (sink + 1) * lanes), slice(part * rows, (part + 1) * rows))
            out_high[(0,) + at] = high
            out_low[(0,) + at] = low


def mix(where, gamma, pattern, mine, theirs, cores):
    operators, spins = gamma.shape[1:3]
    cols, rows = mine.shape[-2:]
    lanes = mine.shape[0] * cols
    sinks = spins // cores
    out = jax.ShapeDtypeStruct((operators, sinks * lanes, 2 * rows), bf16)
    return pl.pallas_call(
        functools.partial(mix_body, cores),
        out_shape=[out, out],
        grid=(operators,),
        in_specs=[SMEM] * 3 + [VMEM] * 2,
        out_specs=[pl.BlockSpec((1,) + out.shape[1:], lambda o: (o, 0, 0))] * 2,
        scratch_shapes=[pltpu.VMEM((3, spins, lanes, rows), f32)],
        cost_estimate=pl.CostEstimate(
            flops=operators * sinks * spins * 8 * lanes * rows,
            bytes_accessed=4 * out.size + 8 * spins * lanes * rows,
            transcendentals=0,
        ),
        compiler_params=pltpu.CompilerParams(vmem_limit_bytes=12 << 20, dimension_semantics=("arbitrary",)),
    )(where, gamma, pattern, mine, theirs)


def phase(turns, chips, table):
    value = f32(table[0])
    for step in range(1, chips):
        value = jnp.where(turns == step, f32(table[step]), value)
    return value


def products_body(chips, cores, tables, where, directions, momenta, mine, theirs, *rest):
    far = rest[: chips - 1]
    far_other = rest[chips - 1 : 2 * (chips - 1)]
    mixed = rest[2 * (chips - 1) : -6]
    out, planes, e_high, e_low, staged, sems = rest[-6:]
    kinds, _, rows, width = mine.shape
    row_count = cores * rows
    operators = mixed[0].shape[0]
    sinks = out.shape[3]
    lanes = out.shape[5]
    depth_rows = width // chips

    for away in range(chips):
        plane = where[2] ^ away
        for kind in range(kinds):
            for part in range(2):
                for core in range(cores):
                    at = slice(core * rows, (core + 1) * rows)
                    if away == 0:
                        value = (mine, theirs)[core][kind, part]
                    else:
                        value = (far, far_other)[core][away - 1][kind, part]
                    planes[plane, kind, part, at] = value

    lane = lax.broadcasted_iota(jnp.int32, (row_count, width), 1)
    copies = []
    for operator in range(operators):
        kind = directions[operator]
        real = planes[0, kind, 0]
        imag = planes[0, kind, 1]
        for plane in range(1, chips):
            turns = lax.rem(momenta[operator] * plane, chips)
            cosine = phase(turns, chips, tables[0])
            sine = phase(turns, chips, tables[1])
            p_real = planes[plane, kind, 0]
            p_imag = planes[plane, kind, 1]
            real = real + (cosine * p_real + sine * p_imag)
            imag = imag + (cosine * p_imag - sine * p_real)
        bit = 1
        while bit < chips:
            reach = bit * depth_rows
            turned = []
            for value in (real, imag):
                up = pltpu.roll(value, width - reach, 1)
                down = up if 2 * reach == width else pltpu.roll(value, reach, 1)
                swapped = jnp.where((lane & reach) == 0, up, down)
                turned.append(jnp.where((where[2] & bit) != 0, swapped, value))
            real, imag = turned
            bit *= 2
        right_col = depth_rows
        for value, spots in ((real, ((0, 0, 1), (row_count, right_col, 1))), (imag, ((row_count, 0, 1), (0, right_col, -1)))):
            for scratch, piece in zip((e_high, e_low), cut(value)):
                for away in range(chips):
                    part = piece[:, away * depth_rows : (away + 1) * depth_rows]
                    for row, col, sign in spots:
                        scratch[operator, away, row : row + row_count, col : col + depth_rows] = part if sign > 0 else -part
        result = None
        for away in range(chips):
            left = (e_high[operator, away], e_low[operator, away])
            right = (mixed[2 * away][operator], mixed[2 * away + 1][operator])
            term = three_pass(left, right, ((1,), (1,)))
            result = term if result is None else result + term
        for part in range(2):
            for core in range(cores):
                row = pl.multiple_of((where[3] ^ core) * rows, rows)
                for sink in range(sinks):
                    staged[operator, part, sink, pl.ds(row, rows), :] = result[
                        part * row_count + core * rows : part * row_count + (core + 1) * rows,
                        sink * lanes : (sink + 1) * lanes,
                    ]
        copies.append(pltpu.make_async_copy(staged.at[operator], out.at[:, operator, 0], sems.at[operator]))
        copies[-1].start()
    for copy in copies:
        copy.wait()


def products(where, directions, momenta, mine, theirs, far, far_other, mixed, shape, chips, cores):
    kinds, width = mine.shape[0], mine.shape[3]
    rows = cores * mine.shape[2]
    tables = [
        [float(v) for v in fn(np.arange(chips, dtype=np.float32) * np.float32(2.0 * math.pi / chips))]
        for fn in (np.cos, np.sin)
    ]
    operands = [where, directions, momenta, mine, theirs, *far, *far_other, *mixed]
    return pl.pallas_call(
        functools.partial(products_body, chips, cores, tables),
        out_shape=jax.ShapeDtypeStruct(shape, f32),
        in_specs=[SMEM] * 3 + [VMEM] * (len(operands) - 3),
        out_specs=HBM,
        scratch_shapes=[
            pltpu.VMEM((chips, kinds, 2, rows, width), f32),
            pltpu.VMEM((shape[1], chips, 2 * rows, 2 * width // chips), bf16),
            pltpu.VMEM((shape[1], chips, 2 * rows, 2 * width // chips), bf16),
            pltpu.VMEM((shape[1], 2) + shape[3:], f32),
            pltpu.SemaphoreType.DMA((shape[1],)),
        ],
        name="products",
        cost_estimate=pl.CostEstimate(
            flops=3 * 2 * shape[1] * shape[3] * 2 * rows * 2 * width * shape[5],
            bytes_accessed=4 * math.prod(shape),
            transcendentals=0,
        ),
        compiler_params=pltpu.CompilerParams(vmem_limit_bytes=24 << 20),
    )(*operands)


def program(eigenvectors, displaced, perambulators, gamma_values, spin_pattern, directions, momenta):
    width = eigenvectors.shape[4]
    operators = gamma_values.shape[1]
    spins = gamma_values.shape[2]
    times = lax.axis_size("tm")
    chips = lax.axis_size("space")
    cores = lax.axis_size("spin")
    where = place(("parts", "tm", "space", "spin"))

    first = [d for d in range(times) if d == 0 or d % 2]
    later = [d for d in range(times) if d not in first]
    v_other = partner(eigenvectors, "spin", 1)
    d_other = partner(displaced, "spin", 1)
    together, *blocks = pack(where, jnp.swapaxes(perambulators, 3, 4), first)
    crossed = [partner(together, "space", away) for away in range(1, chips)]
    early = {}
    for d in range(1, times):
        early[d] = partner(blocks[d], "tm", d)
    own, other = sums(where, eigenvectors, displaced, v_other, d_other, chips, cores)
    far = [partner(other[:, away - 1], "space", away) for away in range(1, chips)]
    theirs = partner(own, "spin", 1)
    far_other = [partner(value, "spin", 1) for value in far]

    gathered = {}
    for d in first[1:]:
        gathered[d] = [partner(value[first.index(d)], "tm", d) for value in crossed]
    for d in later:
        gathered[d] = [partner(early[d], "space", away) for away in range(1, chips)]
    gathered[0] = [value[0] for value in crossed]
    mixed = []
    for away in range(chips):
        if away == 0:
            here = jnp.stack([blocks[0]] + [early[d] for d in range(1, times)])
        else:
            here = jnp.stack([gathered[d][away - 1] for d in range(times)])
        there = partner(here, "spin", 1)
        mixed += mix(where, gamma_values, spin_pattern, here, there, cores)
    shape = (2, operators, eigenvectors.shape[1], spins // cores, width // chips, perambulators.shape[4] * times)
    return products(where, directions, momenta, own, theirs, far, far_other, mixed, shape, chips, cores)


def solution(mesh):
    in_specs = (
        P(None, ("parts", "tm"), None, ("space", "spin"), None),
        P(None, None, ("parts", "tm"), None, ("space", "spin"), None),
        P(None, "parts", "spin", "space", "tm"),
        P(),
        P(),
        P(),
        P(),
    )
    out_specs = P(None, None, ("parts", "tm"), "spin", "space", None)
    return jax.shard_map(program, mesh=mesh, in_specs=in_specs, out_specs=out_specs, check_vma=False)
```

```python
import functools
import math

import numpy as np

import jax
import jax.numpy as jnp
from jax import lax
from jax.experimental import pallas as pl
from jax.experimental.pallas import tpu as pltpu
from jax.sharding import PartitionSpec as P


f32 = jnp.float32
bf16 = jnp.bfloat16
VMEM = pl.BlockSpec(memory_space=pltpu.VMEM)
SMEM = pl.BlockSpec(memory_space=pltpu.SMEM)
HBM = pl.BlockSpec(memory_space=pltpu.HBM)


def in_hbm(value):
    return pltpu.with_memory_space_constraint(value, pltpu.HBM)


def cut(value):
    high = value.astype(bf16)
    return high, (value - high.astype(f32)).astype(bf16)


def three_pass(left, right, dims):
    def dot(a, b):
        return lax.dot_general(a, b, (dims, ((), ())), preferred_element_type=f32)

    return dot(left[0], right[0]) + dot(left[0], right[1]) + dot(left[1], right[0])


def place(axes):
    return jnp.stack([lax.axis_index(axis) for axis in axes]).astype(jnp.int32)


def partner(value, axis, distance):
    size = lax.axis_size(axis)
    return lax.ppermute(value, axis, [(i, i ^ distance) for i in range(size)])


def pack_body(first, where, peram, together, *rest):
    outs, buffer, sem = rest[:-2], rest[-2], rest[-1]
    copy = pltpu.make_async_copy(peram, buffer, sem)
    copy.start()
    copy.wait()
    for distance, out in enumerate(outs):
        for part in range(buffer.shape[0]):
            block = buffer[part, where[1] ^ distance]
            out[part] = block
            if distance in first:
                together[first.index(distance), part] = block


def pack(where, peram, first):
    parts, times = peram.shape[:2]
    one = (parts,) + peram.shape[2:]
    return pl.pallas_call(
        functools.partial(pack_body, first),
        out_shape=[jax.ShapeDtypeStruct(dims, f32) for dims in [(len(first),) + one] + [one] * times],
        in_specs=[SMEM, HBM],
        out_specs=[VMEM] * (times + 1),
        scratch_shapes=[pltpu.VMEM(peram.shape, f32), pltpu.SemaphoreType.DMA],
        name="pack",
        cost_estimate=pl.CostEstimate(flops=0, bytes_accessed=peram.size * 12, transcendentals=0),
        compiler_params=pltpu.CompilerParams(vmem_limit_bytes=8 << 20),
    )(where, in_hbm(peram))


def sums_body(
    chips, cores, where, vectors, moved, v_other, d_other, own, other, v_buf, d_buf, left_high, left_low, v_sem, d_sem
):
    colours, sites, width = vectors.shape[2:]
    kinds = moved.shape[1]
    depth = colours * sites
    rows = width // (chips * cores)
    kind = pl.program_id(0)

    def v_copy(colour):
        return pltpu.make_async_copy(vectors.at[:, 0, colour], v_buf.at[colour], v_sem.at[colour])

    def d_copy(index):
        return pltpu.make_async_copy(moved.at[:, index, 0], d_buf.at[index], d_sem.at[index])

    @pl.when(kind == 0)
    def _():
        for colour in range(colours):
            v_copy(colour).start()
        for index in range(kinds):
            d_copy(index).start()
        spots = [(chip ^ where[2]) * rows for chip in range(chips)]
        for source in range(cores - 1, -1, -1):
            for colour in range(colours):
                if source == 0:
                    v_copy(colour).wait()
                    pair = v_buf[colour, 0].T, v_buf[colour, 1].T
                else:
                    pair = v_other[0, 0, colour].T, v_other[1, 0, colour].T
                at = source * 2 * depth + colour * sites
                for chip, spot in enumerate(spots):
                    base = chip * cores * rows
                    real, imag = [
                        jnp.where(where[3] == 0, value[base : base + rows], value[base + rows : base + 2 * rows])
                        for value in pair
                    ]
                    for scratch, re, im in zip((left_high, left_low), cut(real), cut(imag)):
                        for part, col, value in ((0, at, re), (0, depth + at, im), (1, at, -im), (1, depth + at, re)):
                            to = pl.multiple_of(part * chips * rows + spot, rows)
                            scratch[pl.ds(to, rows), col : col + sites] = value

    d_copy(kind).wait()
    result = None
    for source in range(cores):
        value = d_buf[kind] if source == 0 else d_other[:, kind, 0]
        at = slice(source * 2 * depth, (source + 1) * 2 * depth)
        term = three_pass((left_high[:, at], left_low[:, at]), cut(value.reshape(2 * depth, width)), ((1,), (0,)))
        result = term if result is None else result + term
    for part in range(2):
        at = part * chips * rows
        own[0, part] = result[at : at + rows]
        for away in range(chips - 1):
            at += rows
            other[0, away, part] = result[at : at + rows]


def sums(where, vectors, displaced, v_other, d_other, chips, cores):
    colours, sites, width = vectors.shape[2:]
    kinds = displaced.shape[1]
    rows = width // (chips * cores)
    depth = 2 * colours * sites
    own = jax.ShapeDtypeStruct((kinds, 2, rows, width), f32)
    other = jax.ShapeDtypeStruct((kinds, chips - 1, 2, rows, width), f32)
    return pl.pallas_call(
        functools.partial(sums_body, chips, cores),
        out_shape=[own, other],
        grid=(kinds,),
        in_specs=[SMEM, HBM, HBM, VMEM, VMEM],
        out_specs=[
            pl.BlockSpec((1,) + own.shape[1:], lambda i: (i, 0, 0, 0)),
            pl.BlockSpec((1,) + other.shape[1:], lambda i: (i, 0, 0, 0, 0)),
        ],
        scratch_shapes=[
            pltpu.VMEM((colours, 2, sites, width), f32),
            pltpu.VMEM((kinds, 2, colours, sites, width), f32),
            pltpu.VMEM((2 * chips * rows, cores * depth), bf16),
            pltpu.VMEM((2 * chips * rows, cores * depth), bf16),
            pltpu.SemaphoreType.DMA((colours,)),
            pltpu.SemaphoreType.DMA((kinds,)),
        ],
        name="sums",
        cost_estimate=pl.CostEstimate(
            flops=12 * width * depth * width * kinds,
            bytes_accessed=4 * (vectors.size + displaced.size) + 4 * kinds * 4 * width * width,
            transcendentals=0,
        ),
        compiler_params=pltpu.CompilerParams(vmem_limit_bytes=20 << 20, dimension_semantics=("arbitrary",)),
    )(where, in_hbm(vectors), in_hbm(displaced), v_other, d_other)


def spread_out(blocks, spread):
    per_core = blocks[0].shape[2]
    for step in range(blocks[0].shape[0]):
        for core, block in enumerate(blocks):
            for spin in range(per_core):
                real = block[step, 0, spin]
                imag = block[step, 1, spin]
                for part, value in enumerate((real, imag, real + imag)):
                    spread[step, part, core * per_core + spin] = value


def mix_one(steps, where, gamma, pattern, operator, spread, out_high, out_low):
    spins, cols, rows = spread.shape[2:]
    sinks = out_high.shape[1]
    cores = spins // sinks
    for index, step in enumerate(steps):
        place = pl.ds(pl.multiple_of((where[1] ^ step) * cols, cols), cols)
        for sink in range(sinks):
            row = where[3] * sinks + sink
            totals = [None] * 3
            for core in range(cores):
                for spin in range(sinks):
                    source = (where[3] ^ core) * sinks + spin
                    on = pattern[operator, row, source].astype(f32)
                    a = gamma[0, operator, row, source] * on
                    b = gamma[1, operator, row, source] * on
                    for total, (factor, part) in enumerate(((a, 2), (b - a, 0), (a + b, 1))):
                        term = factor * spread[index, part, core * sinks + spin]
                        totals[total] = term if totals[total] is None else totals[total] + term
            for part, value in enumerate((totals[0] - totals[2], totals[0] + totals[1])):
                high, low = cut(value)
                out_high[operator, sink, place, part * rows : (part + 1) * rows] = high
                out_low[operator, sink, place, part * rows : (part + 1) * rows] = low


def mix_body(steps, where, gamma, pattern, mine, theirs, out_high, out_low, spread):
    spread_out((mine, theirs), spread)

    def one(operator, carry):
        mix_one(steps, where, gamma, pattern, operator, spread, out_high, out_low)
        return carry

    lax.fori_loop(0, gamma.shape[1], one, 0)


def mix(where, gamma, pattern, mine, theirs, steps, times, cores):
    operators, spins = gamma.shape[1:3]
    count, _, _, cols, rows = mine.shape
    sinks = spins // cores
    out = jax.ShapeDtypeStruct((operators, sinks, times * cols, 2 * rows), bf16)
    return pl.pallas_call(
        functools.partial(mix_body, steps),
        out_shape=[out, out],
        in_specs=[SMEM] * 3 + [VMEM] * 2,
        out_specs=[VMEM] * 2,
        scratch_shapes=[pltpu.VMEM((count, 3, spins, cols, rows), f32)],
        name="mix",
        cost_estimate=pl.CostEstimate(
            flops=operators * sinks * spins * 8 * count * cols * rows,
            bytes_accessed=4 * out.size,
            transcendentals=0,
        ),
        compiler_params=pltpu.CompilerParams(vmem_limit_bytes=8 << 20),
    )(where, gamma, pattern, mine, theirs)


def flat(value):
    return value.reshape((-1,) + value.shape[2:])


def phase(turns, chips, table):
    value = f32(table[0])
    for step in range(1, chips):
        value = jnp.where(turns == step, f32(table[step]), value)
    return value


def products_body(
    chips, cores, steps, tables, where, gamma, pattern, directions, momenta, mine, theirs, near_high, near_low, *rest
):
    away_count = chips - 1
    far, far_other, late, late_other = [rest[i * away_count : (i + 1) * away_count] for i in range(4)]
    rest = rest[6 * away_count :]
    out, mixed, rest = rest[0], rest[1 : 1 + 2 * away_count], rest[1 + 2 * away_count :]
    planes, e_high, e_low, spread, staged, sems = rest
    kinds, _, rows, width = mine.shape
    row_count = cores * rows
    operators = near_high.shape[0]
    sinks = out.shape[3]
    lanes = out.shape[5]
    depth_rows = width // chips

    for index in range(away_count):
        spread_out((late[index], late_other[index]), spread.at[index])

    def mix_late(operator):
        for index in range(away_count):
            mix_one(steps, where, gamma, pattern, operator, spread.at[index], mixed[2 * index], mixed[2 * index + 1])

    mix_late(0)
    for away in range(chips):
        plane = where[2] ^ away
        for kind in range(kinds):
            for part in range(2):
                for core in range(cores):
                    at = slice(core * rows, (core + 1) * rows)
                    if away == 0:
                        value = (mine, theirs)[core][kind, part]
                    else:
                        value = (far, far_other)[core][away - 1][kind, part]
                    planes[plane, kind, part, at] = value

    lane = lax.broadcasted_iota(jnp.int32, (row_count, width), 1)
    copies = []
    for operator in range(operators):
        kind = directions[operator]
        real = planes[0, kind, 0]
        imag = planes[0, kind, 1]
        for plane in range(1, chips):
            turns = lax.rem(momenta[operator] * plane, chips)
            cosine = phase(turns, chips, tables[0])
            sine = phase(turns, chips, tables[1])
            p_real = planes[plane, kind, 0]
            p_imag = planes[plane, kind, 1]
            real = real + (cosine * p_real + sine * p_imag)
            imag = imag + (cosine * p_imag - sine * p_real)
        bit = 1
        while bit < chips:
            reach = bit * depth_rows
            turned = []
            for value in (real, imag):
                up = pltpu.roll(value, width - reach, 1)
                down = up if 2 * reach == width else pltpu.roll(value, reach, 1)
                swapped = jnp.where((lane & reach) == 0, up, down)
                turned.append(jnp.where((where[2] & bit) != 0, swapped, value))
            real, imag = turned
            bit *= 2
        right_col = depth_rows
        for value, spots in ((real, ((0, 0, 1), (row_count, right_col, 1))), (imag, ((row_count, 0, 1), (0, right_col, -1)))):
            for scratch, piece in zip((e_high, e_low), cut(value)):
                for away in range(chips):
                    part = piece[:, away * depth_rows : (away + 1) * depth_rows]
                    for row, col, sign in spots:
                        scratch[operator, away, row : row + row_count, col : col + depth_rows] = part if sign > 0 else -part
        if operator + 1 < operators:
            mix_late(operator + 1)
        result = None
        for away in range(chips):
            left = (e_high[operator, away], e_low[operator, away])
            if away == 0:
                right = (near_high, near_low)
            else:
                right = mixed[2 * away - 2 : 2 * away]
            right = [flat(value[operator]) for value in right]
            term = three_pass(left, right, ((1,), (1,)))
            result = term if result is None else result + term
        for part in range(2):
            for core in range(cores):
                row = pl.multiple_of((where[3] ^ core) * rows, rows)
                for sink in range(sinks):
                    staged[operator, part, sink, pl.ds(row, rows), :] = result[
                        part * row_count + core * rows : part * row_count + (core + 1) * rows,
                        sink * lanes : (sink + 1) * lanes,
                    ]
        copies.append(pltpu.make_async_copy(staged.at[operator], out.at[:, operator, 0], sems.at[operator]))
        copies[-1].start()
    for copy in copies:
        copy.wait()


def products(where, scalars, mine, theirs, near, far, far_other, late, late_other, mixed, steps, shape, chips, cores):
    kinds, _, rows, width = mine.shape
    spins = scalars[0].shape[2]
    cols, depth_rows = late[0].shape[3:]
    left = pltpu.VMEM((shape[1], chips, 2 * cores * rows, 2 * depth_rows), bf16)
    tables = [
        [float(v) for v in fn(np.arange(chips, dtype=np.float32) * np.float32(2.0 * math.pi / chips))]
        for fn in (np.cos, np.sin)
    ]
    operands = [where, *scalars, mine, theirs, *near, *far, *far_other, *late, *late_other, *mixed]
    outs = [jax.ShapeDtypeStruct(shape, f32)] + [jax.ShapeDtypeStruct(v.shape, v.dtype) for v in mixed]
    return pl.pallas_call(
        functools.partial(products_body, chips, cores, steps, tables),
        out_shape=outs,
        in_specs=[SMEM] * 5 + [VMEM] * (len(operands) - 5),
        out_specs=[HBM] + [VMEM] * len(mixed),
        input_output_aliases={len(operands) - len(mixed) + i: 1 + i for i in range(len(mixed))},
        scratch_shapes=[
            pltpu.VMEM((chips, kinds, 2, cores * rows, width), f32),
            left,
            left,
            pltpu.VMEM((chips - 1, len(steps), 3, spins, cols, depth_rows), f32),
            pltpu.VMEM((shape[1], 2) + shape[3:], f32),
            pltpu.SemaphoreType.DMA((shape[1],)),
        ],
        name="products",
        cost_estimate=pl.CostEstimate(
            flops=3 * 2 * shape[1] * shape[3] * 2 * shape[4] * 2 * width * shape[5],
            bytes_accessed=4 * math.prod(shape),
            transcendentals=0,
        ),
        compiler_params=pltpu.CompilerParams(vmem_limit_bytes=24 << 20),
    )(*operands)[0]


def program(eigenvectors, displaced, perambulators, gamma_values, spin_pattern, directions, momenta):
    width = eigenvectors.shape[4]
    operators = gamma_values.shape[1]
    spins = gamma_values.shape[2]
    times = lax.axis_size("tm")
    chips = lax.axis_size("space")
    cores = lax.axis_size("spin")
    where = place(("parts", "tm", "space", "spin"))

    first = [d for d in range(times) if d == 0 or d % 2]
    later = [d for d in range(times) if d not in first]
    v_other = partner(eigenvectors, "spin", 1)
    d_other = partner(displaced, "spin", 1)
    together, *blocks = pack(where, jnp.swapaxes(perambulators, 3, 4), first)
    crossed = [partner(together, "space", away) for away in range(1, chips)]
    early = {}
    for d in range(1, times):
        early[d] = partner(blocks[d], "tm", d)
    own, other = sums(where, eigenvectors, displaced, v_other, d_other, chips, cores)
    far = [partner(other[:, away - 1], "space", away) for away in range(1, chips)]
    theirs = partner(own, "spin", 1)
    far_other = [partner(value, "spin", 1) for value in far]

    gathered = {}
    for d in first[1:]:
        gathered[d] = [partner(value[first.index(d)], "tm", d) for value in crossed]
    for d in later:
        gathered[d] = [partner(early[d], "space", away) for away in range(1, chips)]
    gathered[0] = [value[0] for value in crossed]
    here = jnp.stack([blocks[0]] + [early[d] for d in range(1, times)])
    there = partner(here, "spin", 1)
    mixing = functools.partial(mix, where, gamma_values, spin_pattern)
    near = mixing(here, there, tuple(range(times)), times, cores)
    mixed, late, late_other = [], [], []
    for away in range(chips - 1):
        here = jnp.stack([gathered[d][away] for d in first])
        there = partner(here, "spin", 1)
        mixed += mixing(here, there, tuple(first), times, cores)
        late.append(jnp.stack([gathered[d][away] for d in later]))
        late_other.append(partner(late[-1], "spin", 1))
    scalars = [gamma_values, spin_pattern, directions, momenta]
    shape = (2, operators, eigenvectors.shape[1], spins // cores, width // chips, perambulators.shape[4] * times)
    return products(
        where, scalars, own, theirs, near, far, far_other, late, late_other, mixed, tuple(later), shape, chips, cores
    )


def solution(mesh):
    in_specs = (
        P(None, ("parts", "tm"), None, ("space", "spin"), None),
        P(None, None, ("parts", "tm"), None, ("space", "spin"), None),
        P(None, "parts", "spin", "space", "tm"),
        P(),
        P(),
        P(),
        P(),
    )
    out_specs = P(None, None, ("parts", "tm"), "spin", "space", None)
    return jax.shard_map(program, mesh=mesh, in_specs=in_specs, out_specs=out_specs, check_vma=False)
```

```python
import functools
import math

import numpy as np

import jax
import jax.numpy as jnp
from jax import lax
from jax.experimental import pallas as pl
from jax.experimental.pallas import tpu as pltpu
from jax.sharding import PartitionSpec as P


f32 = jnp.float32
bf16 = jnp.bfloat16
VMEM = pl.BlockSpec(memory_space=pltpu.VMEM)
SMEM = pl.BlockSpec(memory_space=pltpu.SMEM)
HBM = pl.BlockSpec(memory_space=pltpu.HBM)


def in_hbm(value):
    return pltpu.with_memory_space_constraint(value, pltpu.HBM)


def cut(value):
    high = value.astype(bf16)
    return high, (value - high.astype(f32)).astype(bf16)


def three_pass(left, right, dims):
    def dot(a, b):
        return lax.dot_general(a, b, (dims, ((), ())), preferred_element_type=f32)

    return dot(left[0], right[0]) + dot(left[0], right[1]) + dot(left[1], right[0])


def place(axes):
    return jnp.stack([lax.axis_index(axis) for axis in axes]).astype(jnp.int32)


def partner(value, axis, distance):
    size = lax.axis_size(axis)
    return lax.ppermute(value, axis, [(i, i ^ distance) for i in range(size)])


def pack_body(first, where, peram, together, *rest):
    outs, buffer, sems = rest[:-2], rest[-2], rest[-1]
    copies = [
        pltpu.make_async_copy(peram.at[:, where[1] ^ distance], buffer.at[distance], sems.at[distance])
        for distance in range(len(outs))
    ]
    for copy in copies:
        copy.start()
    for distance, out in enumerate(outs):
        copies[distance].wait()
        out[...] = buffer[distance]
        if distance in first:
            together[first.index(distance)] = buffer[distance]


def pack(where, peram, first):
    parts, times = peram.shape[:2]
    one = (parts,) + peram.shape[2:]
    return pl.pallas_call(
        functools.partial(pack_body, first),
        out_shape=[jax.ShapeDtypeStruct(dims, f32) for dims in [(len(first),) + one] + [one] * times],
        in_specs=[SMEM, HBM],
        out_specs=[VMEM] * (times + 1),
        scratch_shapes=[pltpu.VMEM((times,) + one, f32), pltpu.SemaphoreType.DMA((times,))],
        name="pack",
        cost_estimate=pl.CostEstimate(flops=0, bytes_accessed=peram.size * 12, transcendentals=0),
        compiler_params=pltpu.CompilerParams(vmem_limit_bytes=8 << 20),
    )(where, in_hbm(peram))


def sums_body(
    chips, cores, where, vectors, moved, v_other, d_other, own, other, v_buf, d_buf, left_high, left_low, v_sem, d_sem
):
    colours, sites, width = vectors.shape[2:]
    kinds = moved.shape[1]
    depth = colours * sites
    rows = width // (chips * cores)
    kind = pl.program_id(0)

    def v_copy(colour):
        return pltpu.make_async_copy(vectors.at[:, 0, colour], v_buf.at[colour], v_sem.at[colour])

    def d_copy(index):
        return pltpu.make_async_copy(moved.at[:, index, 0], d_buf.at[index], d_sem.at[index])

    @pl.when(kind == 0)
    def _():
        for colour in range(colours):
            v_copy(colour).start()
        for index in range(kinds):
            d_copy(index).start()
        spots = [(chip ^ where[2]) * rows for chip in range(chips)]
        for source in range(cores - 1, -1, -1):
            for colour in range(colours):
                if source == 0:
                    v_copy(colour).wait()
                    pair = v_buf[colour, 0].T, v_buf[colour, 1].T
                else:
                    pair = v_other[0, 0, colour].T, v_other[1, 0, colour].T
                at = source * 2 * depth + colour * sites
                for chip, spot in enumerate(spots):
                    base = chip * cores * rows
                    real, imag = [
                        jnp.where(where[3] == 0, value[base : base + rows], value[base + rows : base + 2 * rows])
                        for value in pair
                    ]
                    for scratch, re, im in zip((left_high, left_low), cut(real), cut(imag)):
                        for part, col, value in ((0, at, re), (0, depth + at, im), (1, at, -im), (1, depth + at, re)):
                            to = pl.multiple_of(part * chips * rows + spot, rows)
                            scratch[pl.ds(to, rows), col : col + sites] = value

    d_copy(kind).wait()
    result = None
    for source in range(cores):
        value = d_buf[kind] if source == 0 else d_other[:, kind, 0]
        at = slice(source * 2 * depth, (source + 1) * 2 * depth)
        term = three_pass((left_high[:, at], left_low[:, at]), cut(value.reshape(2 * depth, width)), ((1,), (0,)))
        result = term if result is None else result + term
    for part in range(2):
        at = part * chips * rows
        own[0, part] = result[at : at + rows]
        for away in range(chips - 1):
            at += rows
            other[0, away, part] = result[at : at + rows]


def sums(where, vectors, displaced, v_other, d_other, chips, cores):
    colours, sites, width = vectors.shape[2:]
    kinds = displaced.shape[1]
    rows = width // (chips * cores)
    depth = 2 * colours * sites
    own = jax.ShapeDtypeStruct((kinds, 2, rows, width), f32)
    other = jax.ShapeDtypeStruct((kinds, chips - 1, 2, rows, width), f32)
    return pl.pallas_call(
        functools.partial(sums_body, chips, cores),
        out_shape=[own, other],
        grid=(kinds,),
        in_specs=[SMEM, HBM, HBM, VMEM, VMEM],
        out_specs=[
            pl.BlockSpec((1,) + own.shape[1:], lambda i: (i, 0, 0, 0)),
            pl.BlockSpec((1,) + other.shape[1:], lambda i: (i, 0, 0, 0, 0)),
        ],
        scratch_shapes=[
            pltpu.VMEM((colours, 2, sites, width), f32),
            pltpu.VMEM((kinds, 2, colours, sites, width), f32),
            pltpu.VMEM((2 * chips * rows, cores * depth), bf16),
            pltpu.VMEM((2 * chips * rows, cores * depth), bf16),
            pltpu.SemaphoreType.DMA((colours,)),
            pltpu.SemaphoreType.DMA((kinds,)),
        ],
        name="sums",
        cost_estimate=pl.CostEstimate(
            flops=12 * width * depth * width * kinds,
            bytes_accessed=4 * (vectors.size + displaced.size) + 4 * kinds * 4 * width * width,
            transcendentals=0,
        ),
        compiler_params=pltpu.CompilerParams(vmem_limit_bytes=20 << 20, dimension_semantics=("arbitrary",)),
    )(where, in_hbm(vectors), in_hbm(displaced), v_other, d_other)


def spread_out(blocks, spread):
    per_core = blocks[0].shape[2]
    for step in range(blocks[0].shape[0]):
        for core, block in enumerate(blocks):
            for spin in range(per_core):
                real = block[step, 0, spin]
                imag = block[step, 1, spin]
                for part, value in enumerate((real, imag, real + imag)):
                    spread[step, part, core * per_core + spin] = value


def mix_one(steps, where, gamma, pattern, operator, spread, out_high, out_low):
    spins, cols, rows = spread.shape[2:]
    sinks = out_high.shape[1]
    cores = spins // sinks
    for index, step in enumerate(steps):
        place = pl.ds(pl.multiple_of((where[1] ^ step) * cols, cols), cols)
        for sink in range(sinks):
            row = where[3] * sinks + sink
            totals = [None] * 3
            for core in range(cores):
                for spin in range(sinks):
                    source = (where[3] ^ core) * sinks + spin
                    on = pattern[operator, row, source].astype(f32)
                    a = gamma[0, operator, row, source] * on
                    b = gamma[1, operator, row, source] * on
                    for total, (factor, part) in enumerate(((a, 2), (b - a, 0), (a + b, 1))):
                        term = factor * spread[index, part, core * sinks + spin]
                        totals[total] = term if totals[total] is None else totals[total] + term
            for part, value in enumerate((totals[0] - totals[2], totals[0] + totals[1])):
                high, low = cut(value)
                out_high[operator, sink, place, part * rows : (part + 1) * rows] = high
                out_low[operator, sink, place, part * rows : (part + 1) * rows] = low


def mix_body(steps, where, gamma, pattern, mine, theirs, out_high, out_low, spread):
    spread_out((mine, theirs), spread)

    def one(operator, carry):
        mix_one(steps, where, gamma, pattern, operator, spread, out_high, out_low)
        return carry

    lax.fori_loop(0, gamma.shape[1], one, 0)


def mix(where, gamma, pattern, mine, theirs, steps, times, cores):
    operators, spins = gamma.shape[1:3]
    count, _, _, cols, rows = mine.shape
    sinks = spins // cores
    out = jax.ShapeDtypeStruct((operators, sinks, times * cols, 2 * rows), bf16)
    return pl.pallas_call(
        functools.partial(mix_body, steps),
        out_shape=[out, out],
        in_specs=[SMEM] * 3 + [VMEM] * 2,
        out_specs=[VMEM] * 2,
        scratch_shapes=[pltpu.VMEM((count, 3, spins, cols, rows), f32)],
        name="mix",
        cost_estimate=pl.CostEstimate(
            flops=operators * sinks * spins * 8 * count * cols * rows,
            bytes_accessed=4 * out.size,
            transcendentals=0,
        ),
        compiler_params=pltpu.CompilerParams(vmem_limit_bytes=8 << 20),
    )(where, gamma, pattern, mine, theirs)


def flat(value):
    return value.reshape((-1,) + value.shape[2:])


def phase(turns, chips, table):
    value = f32(table[0])
    for step in range(1, chips):
        value = jnp.where(turns == step, f32(table[step]), value)
    return value


def products_body(
    chips, cores, steps, tables, where, gamma, pattern, directions, momenta, mine, theirs, near_high, near_low, *rest
):
    away_count = chips - 1
    far, far_other, late, late_other = [rest[i * away_count : (i + 1) * away_count] for i in range(4)]
    rest = rest[6 * away_count :]
    out, mixed, rest = rest[0], rest[1 : 1 + 2 * away_count], rest[1 + 2 * away_count :]
    planes, e_high, e_low, spread, staged, sems = rest
    kinds, _, rows, width = mine.shape
    row_count = cores * rows
    operators = near_high.shape[0]
    sinks = out.shape[3]
    lanes = out.shape[5]
    depth_rows = width // chips

    for index in range(away_count):
        spread_out((late[index], late_other[index]), spread.at[index])

    def mix_late(operator):
        for index in range(away_count):
            mix_one(steps, where, gamma, pattern, operator, spread.at[index], mixed[2 * index], mixed[2 * index + 1])

    mix_late(0)
    for away in range(chips):
        plane = where[2] ^ away
        for kind in range(kinds):
            for part in range(2):
                for core in range(cores):
                    at = slice(core * rows, (core + 1) * rows)
                    if away == 0:
                        value = (mine, theirs)[core][kind, part]
                    else:
                        value = (far, far_other)[core][away - 1][kind, part]
                    planes[plane, kind, part, at] = value

    lane = lax.broadcasted_iota(jnp.int32, (row_count, width), 1)
    copies = []
    for operator in range(operators):
        kind = directions[operator]
        real = planes[0, kind, 0]
        imag = planes[0, kind, 1]
        for plane in range(1, chips):
            turns = lax.rem(momenta[operator] * plane, chips)
            cosine = phase(turns, chips, tables[0])
            sine = phase(turns, chips, tables[1])
            p_real = planes[plane, kind, 0]
            p_imag = planes[plane, kind, 1]
            real = real + (cosine * p_real + sine * p_imag)
            imag = imag + (cosine * p_imag - sine * p_real)
        bit = 1
        while bit < chips:
            reach = bit * depth_rows
            turned = []
            for value in (real, imag):
                up = pltpu.roll(value, width - reach, 1)
                down = up if 2 * reach == width else pltpu.roll(value, reach, 1)
                swapped = jnp.where((lane & reach) == 0, up, down)
                turned.append(jnp.where((where[2] & bit) != 0, swapped, value))
            real, imag = turned
            bit *= 2
        right_col = depth_rows
        for value, spots in ((real, ((0, 0, 1), (row_count, right_col, 1))), (imag, ((row_count, 0, 1), (0, right_col, -1)))):
            for scratch, piece in zip((e_high, e_low), cut(value)):
                for away in range(chips):
                    part = piece[:, away * depth_rows : (away + 1) * depth_rows]
                    for row, col, sign in spots:
                        scratch[operator, away, row : row + row_count, col : col + depth_rows] = part if sign > 0 else -part
        if operator + 1 < operators:
            mix_late(operator + 1)
        result = None
        for away in range(chips):
            left = (e_high[operator, away], e_low[operator, away])
            if away == 0:
                right = (near_high, near_low)
            else:
                right = mixed[2 * away - 2 : 2 * away]
            right = [flat(value[operator]) for value in right]
            term = three_pass(left, right, ((1,), (1,)))
            result = term if result is None else result + term
        for part in range(2):
            for core in range(cores):
                row = pl.multiple_of((where[3] ^ core) * rows, rows)
                for sink in range(sinks):
                    staged[operator, part, sink, pl.ds(row, rows), :] = result[
                        part * row_count + core * rows : part * row_count + (core + 1) * rows,
                        sink * lanes : (sink + 1) * lanes,
                    ]
            copies.append(
                pltpu.make_async_copy(staged.at[operator, part], out.at[part, operator, 0], sems.at[operator, part])
            )
            copies[-1].start()
    for copy in copies:
        copy.wait()


def products(where, scalars, mine, theirs, near, far, far_other, late, late_other, mixed, steps, shape, chips, cores):
    kinds, _, rows, width = mine.shape
    spins = scalars[0].shape[2]
    cols, depth_rows = late[0].shape[3:]
    left = pltpu.VMEM((shape[1], chips, 2 * cores * rows, 2 * depth_rows), bf16)
    tables = [
        [float(v) for v in fn(np.arange(chips, dtype=np.float32) * np.float32(2.0 * math.pi / chips))]
        for fn in (np.cos, np.sin)
    ]
    operands = [where, *scalars, mine, theirs, *near, *far, *far_other, *late, *late_other, *mixed]
    outs = [jax.ShapeDtypeStruct(shape, f32)] + [jax.ShapeDtypeStruct(v.shape, v.dtype) for v in mixed]
    return pl.pallas_call(
        functools.partial(products_body, chips, cores, steps, tables),
        out_shape=outs,
        in_specs=[SMEM] * 5 + [VMEM] * (len(operands) - 5),
        out_specs=[HBM] + [VMEM] * len(mixed),
        input_output_aliases={len(operands) - len(mixed) + i: 1 + i for i in range(len(mixed))},
        scratch_shapes=[
            pltpu.VMEM((chips, kinds, 2, cores * rows, width), f32),
            left,
            left,
            pltpu.VMEM((chips - 1, len(steps), 3, spins, cols, depth_rows), f32),
            pltpu.VMEM((shape[1], 2) + shape[3:], f32),
            pltpu.SemaphoreType.DMA((shape[1], 2)),
        ],
        name="products",
        cost_estimate=pl.CostEstimate(
            flops=3 * 2 * shape[1] * shape[3] * 2 * shape[4] * 2 * width * shape[5],
            bytes_accessed=4 * math.prod(shape),
            transcendentals=0,
        ),
        compiler_params=pltpu.CompilerParams(vmem_limit_bytes=24 << 20),
    )(*operands)[0]


def program(eigenvectors, displaced, perambulators, gamma_values, spin_pattern, directions, momenta):
    width = eigenvectors.shape[4]
    operators = gamma_values.shape[1]
    spins = gamma_values.shape[2]
    times = lax.axis_size("tm")
    chips = lax.axis_size("space")
    cores = lax.axis_size("spin")
    where = place(("parts", "tm", "space", "spin"))

    first = [d for d in range(times) if d == 0 or d % 2]
    later = [d for d in range(times) if d not in first]
    v_other = partner(eigenvectors, "spin", 1)
    d_other = partner(displaced, "spin", 1)
    together, *blocks = pack(where, jnp.swapaxes(perambulators, 3, 4), first)
    crossed = [partner(together, "space", away) for away in range(1, chips)]
    early = {}
    for d in range(1, times):
        early[d] = partner(blocks[d], "tm", d)
    own, other = sums(where, eigenvectors, displaced, v_other, d_other, chips, cores)
    far = [partner(other[:, away - 1], "space", away) for away in range(1, chips)]
    theirs = partner(own, "spin", 1)
    far_other = [partner(value, "spin", 1) for value in far]

    gathered = {}
    for d in first[1:]:
        gathered[d] = [partner(value[first.index(d)], "tm", d) for value in crossed]
    for d in later:
        gathered[d] = [partner(early[d], "space", away) for away in range(1, chips)]
    gathered[0] = [value[0] for value in crossed]
    here = jnp.stack([blocks[0]] + [early[d] for d in range(1, times)])
    there = partner(here, "spin", 1)
    mixing = functools.partial(mix, where, gamma_values, spin_pattern)
    near = mixing(here, there, tuple(range(times)), times, cores)
    mixed, late, late_other = [], [], []
    for away in range(chips - 1):
        here = jnp.stack([gathered[d][away] for d in first])
        there = partner(here, "spin", 1)
        mixed += mixing(here, there, tuple(first), times, cores)
        late.append(jnp.stack([gathered[d][away] for d in later]))
        late_other.append(partner(late[-1], "spin", 1))
    scalars = [gamma_values, spin_pattern, directions, momenta]
    shape = (2, operators, eigenvectors.shape[1], spins // cores, width // chips, perambulators.shape[4] * times)
    return products(
        where, scalars, own, theirs, near, far, far_other, late, late_other, mixed, tuple(later), shape, chips, cores
    )


def solution(mesh):
    in_specs = (
        P(None, ("parts", "tm"), None, ("space", "spin"), None),
        P(None, None, ("parts", "tm"), None, ("space", "spin"), None),
        P(None, "parts", "spin", "space", "tm"),
        P(),
        P(),
        P(),
        P(),
    )
    out_specs = P(None, None, ("parts", "tm"), "spin", "space", None)
    return jax.shard_map(program, mesh=mesh, in_specs=in_specs, out_specs=out_specs, check_vma=False)
```
